512 devices in a mesh: row: 16 (over z), col: 16 (over y_hi, x, core), fr: 2 (over y_lo).
Axes of the slice: x: 4, y: 4 (y_hi: 2, y_lo: 2; y = y_hi * 2 + y_lo), z: 16, core: 2. Of those that a mesh axis runs over, the one named last changes fastest.
Arguments:
- sigma_aa: float32 [12288, 12288], P(('fr', 'row'), 'col'), parts along dimension 0, may hold values from -6 to 6
- l_as: float32 [24576, 6144], P(('fr', 'row'), 'col'), parts along dimension 0, may hold values from -0.078125 to 0.078125
- block_mask: int32 [32, 16], P(('fr', 'row'), 'col'), parts along dimension 0, may hold values 0 or 1
Outputs:
- sigma_as: float32 [12288, 6144], P(('fr', 'row'), 'col'), parts along dimension 0
The draws below stay inside these ranges and needn't reach their ends.
There are 2 independent parts, one for each index of `fr`. The reference program is written for one: setup_inputs(seed, part) draws one part's arguments, and reference() takes and returns one part's arrays. A program takes and returns all parts, laid end to end along the dimension named above; each array names one. Nothing has to cross between parts.
All inputs are finite; a program needn't handle non-finite values. No bound on the sum of `block_mask` on one device may be relied on, other than what follows from the above.
Results may differ from the reference program's by a relative error of at most 0.0003.
Values sent between devices are 32-bit elements; how exact they have to be, the bound alone decides.
A program may use at most 64 MiB of HBM per device.

```python
import jax
import jax.numpy as jnp
from jax import lax

ANC = 12288
SEP = 6144
ROW_DEV = 384
NB = 16
STEPS = 8
ROWS = 6144


def set_ends(array, stream_key, least, largest):
    longest = array.shape.index(max(array.shape))
    spots = []
    for shift in (0, 1):
        where = [jax.random.randint(jax.random.fold_in(stream_key, axis), (), 0, length) for axis, length in enumerate(array.shape)]
        where[longest] = (where[longest] + shift) % array.shape[longest]
        spots.append(tuple(where))
    return array.at[spots[0]].set(least).at[spots[1]].set(largest)


def shard_levels(stream_key, shape, split, smallest, top_value):
    level, own = 1.0, jax.random.fold_in(stream_key, 6)
    for position, shards_of in split:
        draws = jnp.exp(jax.random.uniform(jax.random.fold_in(own, position), (shards_of,), jnp.float32, smallest / len(split), top_value / len(split)))
        level = level * jnp.repeat(draws, shape[position] // shards_of).reshape([-1 if axis == position else 1 for axis in range(len(shape))])
    return level


def normal_values(rng, shape, scale, reach, shards=(), kind=jnp.bfloat16):
    entries = scale * jax.random.normal(rng, shape, jnp.float32)
    if shards:
        entries = entries * shard_levels(rng, shape, shards, -0.22, 0.18)
    return jnp.clip(entries, -reach, reach).astype(kind)


def setup_inputs(seed: int = 0, part: int = 0) -> dict:
    keys = jax.random.split(jax.random.key(seed), 4)
    part_keys = jax.random.split(jax.random.fold_in(keys[3], part), 4)
    sigma_aa = normal_values(part_keys[0], (ROWS, ANC), 1.0, 6.0, ((0, 16), (1, 16)), jnp.float32)
    l_as = normal_values(part_keys[1], (ANC, SEP), (ANC // 2) ** -0.5, 0.078125, ((0, 16), (1, 16)), jnp.float32)
    block_mask = set_ends((jax.random.randint(part_keys[2], (NB, NB), 0, 4) < 3).astype(jnp.int32), jax.random.fold_in(part_keys[2], 1), 0, 1)
    return {"sigma_aa": sigma_aa, "l_as": l_as, "block_mask": block_mask}


def reference(sigma_aa, l_as, block_mask):
    anc_block = ANC // NB
    sep_block = SEP // NB
    mask_full = jnp.repeat(jnp.repeat(block_mask.astype(l_as.dtype), anc_block, 0), sep_block, 1)
    factor = l_as * mask_full
    sigma_blocks = sigma_aa.reshape(NB, ROW_DEV, NB, anc_block)
    factor_blocks = factor.reshape(NB, anc_block, NB, sep_block)
    blocks = jnp.arange(NB, dtype=jnp.int32)

    def one_row(block_row):
        row_panel = sigma_blocks[block_row]
        summed = jnp.zeros((ROW_DEV, NB, sep_block), sigma_aa.dtype)
        for turn in range(STEPS):
            stored_cols = (blocks + turn) % NB
            lhs_block = row_panel[:, stored_cols, :]
            stored_row = (block_row + turn) % NB
            rhs_block = factor_blocks[stored_row]
            summed = summed + jnp.einsum("rja,ajs->rjs", lhs_block, rhs_block, precision=lax.Precision.HIGHEST)
        return -summed

    result = lax.map(one_row, blocks)
    return result.reshape(ROWS, SEP)
```

```python
import functools

import jax
import jax.numpy as jnp
from jax import lax
from jax.experimental import pallas as pl
from jax.experimental.pallas import tpu as pltpu
from jax.sharding import PartitionSpec as P

MESH = pl.DeviceIdType.MESH
F32, BF16 = jnp.float32, jnp.bfloat16

NZ = 16
TURNS = 8
DOWN_HOPS, UP_HOPS = TURNS - 1, NZ - 1
DOWN_ROWS = 528
DOWN_CHUNKS, UP_CHUNKS = 3, 2
TILE = 128


def split(value):
    high = value.astype(BF16)
    return high, (value - high.astype(F32)).astype(BF16)


def kernel(
    sigma_hbm, factor_hbm, mask_ref, out_ref,
    own, other, relay, factor, down, up, rhs_high, rhs_low,
    load_sem, down_send, down_recv, up_send, up_recv,
    y_send, y_recv, x_send, x_recv, pair_send, pair_recv,
):
    rows, inner = sigma_hbm.shape
    half = rows // 2
    up_rows = inner - DOWN_ROWS
    down_chunk, up_chunk = DOWN_ROWS // DOWN_CHUNKS, up_rows // UP_CHUNKS
    z, col, fr = lax.axis_index("row"), lax.axis_index("col"), lax.axis_index("fr")
    core, x, y = col % 2, (col // 2) % 4, (col // 8) * 2 + fr

    def at_z(step):
        return ((z + step + NZ) % NZ, col, fr)

    def at_x(step):
        return (z, (col // 8) * 8 + ((x + step + 4) % 4) * 2 + core, fr)

    def at_y(step):
        there = (y + step + 4) % 4
        return (z, (there // 2) * 8 + x * 2 + core, there % 2)

    sibling = (z, col + 1 - 2 * core, fr)

    sigma_load = pltpu.make_async_copy(sigma_hbm, own.at[0], load_sem.at[0])
    factor_load = pltpu.make_async_copy(factor_hbm, factor, load_sem.at[1])
    factor_load.start()
    sigma_load.start()

    barrier = pltpu.get_barrier_semaphore()
    peers = (at_z(-1), at_z(1), at_y(-1), at_y(1), at_x(1), at_x(2), at_x(3), sibling)
    for peer in peers:
        pl.semaphore_signal(barrier, inc=1, device_id=peer, device_id_type=MESH)

    def send(src, dst, send_sem, recv_sem, peer):
        return pltpu.make_async_remote_copy(
            src_ref=src, dst_ref=dst, send_sem=send_sem, recv_sem=recv_sem,
            device_id=peer, device_id_type=MESH,
        )

    def down_copy(step, piece):
        span = pl.ds(piece * down_chunk, down_chunk)
        source = factor.at[span] if step == 0 else down.at[step - 1, span]
        return send(source, down.at[step, span], down_send.at[step, piece], down_recv.at[step, piece], at_z(-1))

    def up_copy(step, piece):
        span = pl.ds(piece * up_chunk, up_chunk)
        source = factor.at[pl.ds(DOWN_ROWS + piece * up_chunk, up_chunk)] if step == 0 else up.at[step - 1, span]
        return send(source, up.at[step, span], up_send.at[step, piece], up_recv.at[step, piece], at_z(1))

    def y_copy(leg, way):
        span = pl.ds(way * half, half)
        source = own.at[0, span] if leg == 0 else relay.at[way]
        target = relay.at[way] if leg == 0 else own.at[4, span]
        return send(source, target, y_send.at[leg, way], y_recv.at[leg, way], at_y(1 - 2 * way))

    def x_copy(distance):
        which = jnp.where(x >= distance, 0, 4)
        return send(own.at[which], own.at[distance], x_send.at[distance - 1], x_recv.at[distance - 1], at_x(-distance))

    def pair_copy(distance):
        slot = distance - 1 + core
        return send(own.at[distance], other.at[slot], pair_send.at[slot], pair_recv.at[slot], sibling)

    def pair_arrival(slot):
        return send(other.at[slot], other.at[slot], pair_send.at[slot], pair_recv.at[slot], sibling)

    def multiply(turn):
        if turn == 0:
            high, low = split(factor[...])
            rhs_high[...] = high
            rhs_low[...] = low
        else:
            high, low = split(down[turn - 1])
            rhs_high[pl.ds(0, DOWN_ROWS)] = high
            rhs_low[pl.ds(0, DOWN_ROWS)] = low
            high, low = split(up[NZ - 1 - turn])
            rhs_high[pl.ds(DOWN_ROWS, up_rows)] = high
            rhs_low[pl.ds(DOWN_ROWS, up_rows)] = low

        @pl.loop(0, rows // TILE)
        def _(tile):
            span = pl.ds(pl.multiple_of(tile * TILE, TILE), TILE)
            block = own[turn // 2, span] if turn % 2 == 0 else other[turn // 2, span]
            high, low = split(block)
            dot = functools.partial(jnp.dot, preferred_element_type=F32)
            value = dot(high, rhs_high[...]) + (dot(high, rhs_low[...]) + dot(low, rhs_high[...]))
            out_ref[span] = -value if turn == 0 else out_ref[span] - value

    factor_load.wait()
    factor[...] = factor[...] * mask_ref[0, 0].astype(F32)
    sigma_load.wait()
    pl.semaphore_wait(barrier, len(peers))

    for piece in range(max(DOWN_CHUNKS, UP_CHUNKS)):
        if piece < DOWN_CHUNKS:
            down_copy(0, piece).start()
        if piece < UP_CHUNKS:
            up_copy(0, piece).start()
    for way in range(2):
        y_copy(0, way).start()
    for distance in (1, 3, 2):

        @pl.when(x >= distance)
        def _():
            x_copy(distance).start()

    @pl.when(core == 1)
    def _():
        pair_copy(0).start()

    multiply(0)

    def down_event(step, piece):
        down_copy(step, piece).wait_recv()
        if step + 1 < DOWN_HOPS:
            down_copy(step + 1, piece).start()

    def up_event(step, piece):
        up_copy(step, piece).wait_recv()
        if step + 1 < UP_HOPS:
            up_copy(step + 1, piece).start()

    def y_event(leg):
        for way in range(2):
            y_copy(leg, way).wait_recv()
            if leg == 0:
                y_copy(1, way).start()
        if leg == 1:
            for distance in (1, 3, 2):

                @pl.when(x < distance)
                def _():
                    x_copy(distance).start()

            @pl.when(core == 0)
            def _():
                pair_copy(4).start()

    def x_event(distance):
        x_copy(distance).wait_recv()
        pair_copy(distance).start()

    def pair_event():
        for slot in range(4):
            pair_arrival(slot).wait_recv()

    events = [
        (0.14, functools.partial(y_event, 0)),
        (0.28, functools.partial(y_event, 1)),
        (0.55, functools.partial(x_event, 1)),
        (0.56, functools.partial(x_event, 3)),
        (0.72, functools.partial(x_event, 2)),
        (0.745, pair_event),
    ]
    for step in range(DOWN_HOPS):
        for piece in range(DOWN_CHUNKS):
            events.append(((step + (piece + 1) / DOWN_CHUNKS) / DOWN_HOPS, functools.partial(down_event, step, piece)))
    for step in range(UP_HOPS):
        for piece in range(UP_CHUNKS):
            events.append(((step + (piece + 1) / UP_CHUNKS) / UP_HOPS, functools.partial(up_event, step, piece)))
    for turn in range(1, TURNS):
        ready = max(turn / DOWN_HOPS, (NZ - turn) / UP_HOPS)
        events.append((max(ready, 0.75) + 0.001, functools.partial(multiply, turn)))
    for _, event in sorted(events, key=lambda entry: entry[0]):
        event()

    for step in range(DOWN_HOPS):
        for piece in range(DOWN_CHUNKS):
            down_copy(step, piece).wait_send()
    for step in range(UP_HOPS):
        for piece in range(UP_CHUNKS):
            up_copy(step, piece).wait_send()
    for leg in range(2):
        for way in range(2):
            y_copy(leg, way).wait_send()
    for distance in (1, 2, 3):
        x_copy(distance).wait_send()
    for slot in range(4):
        pair_arrival(slot).wait_send()


def body(sigma_aa, l_as, block_mask):
    rows, inner = sigma_aa.shape
    width = l_as.shape[1]
    up_rows = inner - DOWN_ROWS
    dma = pltpu.SemaphoreType.DMA
    return pl.pallas_call(
        kernel,
        out_shape=jax.ShapeDtypeStruct((rows, width), F32),
        in_specs=[
            pl.BlockSpec(memory_space=pl.ANY),
            pl.BlockSpec(memory_space=pl.ANY),
            pl.BlockSpec(memory_space=pltpu.SMEM),
        ],
        out_specs=pl.BlockSpec(memory_space=pltpu.VMEM),
        scratch_shapes=[
            pltpu.VMEM((5, rows, inner), F32),
            pltpu.VMEM((4, rows, inner), F32),
            pltpu.VMEM((2, rows // 2, inner), F32),
            pltpu.VMEM((inner, width), F32),
            pltpu.VMEM((DOWN_HOPS, DOWN_ROWS, width), F32),
            pltpu.VMEM((UP_HOPS, up_rows, width), F32),
            pltpu.VMEM((inner, width), BF16),
            pltpu.VMEM((inner, width), BF16),
            dma((2,)),
            dma((DOWN_HOPS, DOWN_CHUNKS)),
            dma((DOWN_HOPS, DOWN_CHUNKS)),
            dma((UP_HOPS, UP_CHUNKS)),
            dma((UP_HOPS, UP_CHUNKS)),
            dma((2, 2)),
            dma((2, 2)),
            dma((3,)),
            dma((3,)),
            dma((4,)),
            dma((4,)),
        ],
        compiler_params=pltpu.CompilerParams(
            collective_id=0, has_side_effects=True, vmem_limit_bytes=56 << 20
        ),
        name="front_product",
    )(sigma_aa, l_as, block_mask)


def solution(mesh):
    placed = (P(("fr", "row"), "col"), P(("fr", "row"), "col"), P(("fr", "row"), "col"))
    return jax.shard_map(
        body, mesh=mesh, in_specs=placed, out_specs=P(("fr", "row"), "col"), check_vma=False
    )
```

```python
import functools

import jax
import jax.numpy as jnp
from jax import lax
from jax.experimental import pallas as pl
from jax.experimental.pallas import tpu as pltpu
from jax.sharding import PartitionSpec as P

MESH = pl.DeviceIdType.MESH
F32, BF16 = jnp.float32, jnp.bfloat16

NZ = 16
TURNS = 8
DOWN_HOPS, UP_HOPS = TURNS - 1, NZ - 1
DOWN_ROWS = 528
DOWN_CHUNKS, UP_CHUNKS = 3, 2
TILE = 128
AT_Y, AT_X, AT_PAIR = (0.14, 0.28), (0.8, 0.805, 0.81), 0.83


def split(value):
    high = value.astype(BF16)
    return high, (value - high.astype(F32)).astype(BF16)


def kernel(
    sigma_hbm, factor_hbm, mask_ref, out_ref,
    own, other, relay, factor, down, up, rhs_high, rhs_low,
    load_sem, down_send, down_recv, up_send, up_recv,
    y_send, y_recv, x_send, x_recv, pair_send, pair_recv,
):
    rows, inner = sigma_hbm.shape
    half = rows // 2
    up_rows = inner - DOWN_ROWS
    down_chunk, up_chunk = DOWN_ROWS // DOWN_CHUNKS, up_rows // UP_CHUNKS
    z, col, fr = lax.axis_index("row"), lax.axis_index("col"), lax.axis_index("fr")
    core, x, y = col % 2, (col // 2) % 4, (col // 8) * 2 + fr

    def at_z(step):
        return ((z + step + NZ) % NZ, col, fr)

    def at_x(step):
        return (z, (col // 8) * 8 + ((x + step + 4) % 4) * 2 + core, fr)

    def at_y(step):
        there = (y + step + 4) % 4
        return (z, (there // 2) * 8 + x * 2 + core, there % 2)

    sibling = (z, col + 1 - 2 * core, fr)

    sigma_load = pltpu.make_async_copy(sigma_hbm, own.at[0], load_sem.at[0])
    factor_load = pltpu.make_async_copy(factor_hbm, factor, load_sem.at[1])
    factor_load.start()
    sigma_load.start()

    barrier = pltpu.get_barrier_semaphore()
    peers = (at_z(-1), at_z(1), at_y(-1), at_y(1), at_x(1), at_x(2), at_x(3), sibling)
    for peer in peers:
        pl.semaphore_signal(barrier, inc=1, device_id=peer, device_id_type=MESH)

    def send(src, dst, send_sem, recv_sem, peer):
        return pltpu.make_async_remote_copy(
            src_ref=src, dst_ref=dst, send_sem=send_sem, recv_sem=recv_sem,
            device_id=peer, device_id_type=MESH,
        )

    def down_copy(step, piece):
        span = pl.ds((DOWN_CHUNKS - 1 - piece) * down_chunk, down_chunk)
        source = factor.at[span] if step == 0 else down.at[step - 1, span]
        return send(source, down.at[step, span], down_send.at[step, piece], down_recv.at[step, piece], at_z(-1))

    def up_copy(step, piece):
        span = pl.ds(piece * up_chunk, up_chunk)
        source = factor.at[pl.ds(DOWN_ROWS + piece * up_chunk, up_chunk)] if step == 0 else up.at[step - 1, span]
        return send(source, up.at[step, span], up_send.at[step, piece], up_recv.at[step, piece], at_z(1))

    def y_copy(leg, way):
        span = pl.ds(way * half, half)
        source = own.at[0, span] if leg == 0 else relay.at[way]
        target = relay.at[way] if leg == 0 else own.at[4, span]
        return send(source, target, y_send.at[leg, way], y_recv.at[leg, way], at_y(1 - 2 * way))

    def x_copy(distance):
        which = jnp.where(x >= distance, 0, 4)
        return send(own.at[which], own.at[distance], x_send.at[distance - 1], x_recv.at[distance - 1], at_x(-distance))

    def pair_copy(distance):
        slot = distance - 1 + core
        return send(own.at[distance], other.at[slot], pair_send.at[slot], pair_recv.at[slot], sibling)

    def pair_arrival(slot):
        return send(other.at[slot], other.at[slot], pair_send.at[slot], pair_recv.at[slot], sibling)

    def multiply(turn, low_row=0, high_row=None):
        high_row = inner if high_row is None else high_row
        depth, middle = high_row - low_row, min(max(low_row, DOWN_ROWS), high_row)

        def take(source, start, stop, target):
            if stop > start:
                high, low = split(source[pl.ds(start, stop - start)])
                rhs_high[pl.ds(target, stop - start)] = high
                rhs_low[pl.ds(target, stop - start)] = low

        if turn == 0:
            take(factor, low_row, high_row, 0)
        else:
            take(down.at[turn - 1], low_row, middle, 0)
            take(up.at[NZ - 1 - turn], middle - DOWN_ROWS, high_row - DOWN_ROWS, middle - low_row)

        @pl.loop(0, rows // TILE)
        def _(tile):
            span = pl.ds(pl.multiple_of(tile * TILE, TILE), TILE)
            lhs = own if turn % 2 == 0 else other
            high, low = split(lhs[turn // 2, span, pl.ds(low_row, depth)])
            dot = functools.partial(jnp.dot, preferred_element_type=F32)
            one, two = rhs_high[pl.ds(0, depth)], rhs_low[pl.ds(0, depth)]
            value = dot(high, one) + (dot(high, two) + dot(low, one))
            out_ref[span] = -value if turn == 0 else out_ref[span] - value

    factor_load.wait()
    factor[...] = factor[...] * mask_ref[0, 0].astype(F32)
    sigma_load.wait()
    pl.semaphore_wait(barrier, len(peers))

    for piece in range(max(DOWN_CHUNKS, UP_CHUNKS)):
        if piece < DOWN_CHUNKS:
            down_copy(0, piece).start()
        if piece < UP_CHUNKS:
            up_copy(0, piece).start()
    for way in range(2):
        y_copy(0, way).start()
    for distance in (1, 3, 2):

        @pl.when(x >= distance)
        def _():
            x_copy(distance).start()

    @pl.when(core == 1)
    def _():
        pair_copy(0).start()

    multiply(0)

    def down_event(step, piece):
        down_copy(step, piece).wait_recv()
        if step + 1 < DOWN_HOPS:
            down_copy(step + 1, piece).start()

    def up_event(step, piece):
        up_copy(step, piece).wait_recv()
        if step + 1 < UP_HOPS:
            up_copy(step + 1, piece).start()

    def y_event(leg):
        for way in range(2):
            y_copy(leg, way).wait_recv()
            if leg == 0:
                y_copy(1, way).start()
        if leg == 1:
            for distance in (1, 3, 2):

                @pl.when(x < distance)
                def _():
                    x_copy(distance).start()

            @pl.when(core == 0)
            def _():
                pair_copy(4).start()

    def x_event(distance):
        x_copy(distance).wait_recv()
        pair_copy(distance).start()

    def pair_event():
        for slot in range(4):
            pair_arrival(slot).wait_recv()

    whole = DOWN_ROWS * DOWN_HOPS
    events = [(AT_Y[leg], functools.partial(y_event, leg)) for leg in range(2)]
    events += [(when, functools.partial(x_event, distance)) for when, distance in zip(AT_X, (1, 3, 2))]
    events += [(AT_PAIR, pair_event)]
    for step in range(DOWN_HOPS):
        for piece in range(DOWN_CHUNKS):
            when = (step * DOWN_ROWS + (piece + 1) * down_chunk) / whole
            events.append((when, functools.partial(down_event, step, piece)))
    for step in range(UP_HOPS):
        for piece in range(UP_CHUNKS):
            when = (step * up_rows + (piece + 1) * up_chunk) / whole
            events.append((when, functools.partial(up_event, step, piece)))
    last_up = up_rows * UP_HOPS / whole
    products = [(last_up * 0.99, 1, 0, 512), (last_up, 1, 512, inner), (1 - 1 / (DOWN_CHUNKS * DOWN_HOPS), 7, 256, inner), (1, 7, 0, 256)]
    for turn in range(2, TURNS - 1):
        products.append((max(turn * DOWN_ROWS, (NZ - turn) * up_rows) / whole, turn, 0, inner))
    for when, *product in products:
        events.append((max(when, AT_PAIR) + 1e-4, functools.partial(multiply, *product)))
    for _, event in sorted(events, key=lambda entry: entry[0]):
        event()

    for step in range(DOWN_HOPS):
        for piece in range(DOWN_CHUNKS):
            down_copy(step, piece).wait_send()
    for step in range(UP_HOPS):
        for piece in range(UP_CHUNKS):
            up_copy(step, piece).wait_send()
    for leg in range(2):
        for way in range(2):
            y_copy(leg, way).wait_send()
    for distance in (1, 2, 3):
        x_copy(distance).wait_send()
    for slot in range(4):
        pair_arrival(slot).wait_send()


def body(sigma_aa, l_as, block_mask):
    rows, inner = sigma_aa.shape
    width = l_as.shape[1]
    up_rows = inner - DOWN_ROWS
    dma = pltpu.SemaphoreType.DMA
    return pl.pallas_call(
        kernel,
        out_shape=jax.ShapeDtypeStruct((rows, width), F32),
        in_specs=[
            pl.BlockSpec(memory_space=pltpu.HBM),
            pl.BlockSpec(memory_space=pltpu.HBM),
            pl.BlockSpec(memory_space=pltpu.SMEM),
        ],
        out_specs=pl.BlockSpec(memory_space=pltpu.VMEM),
        scratch_shapes=[
            pltpu.VMEM((5, rows, inner), F32),
            pltpu.VMEM((4, rows, inner), F32),
            pltpu.VMEM((2, rows // 2, inner), F32),
            pltpu.VMEM((inner, width), F32),
            pltpu.VMEM((DOWN_HOPS, DOWN_ROWS, width), F32),
            pltpu.VMEM((UP_HOPS, up_rows, width), F32),
            pltpu.VMEM((inner, width), BF16),
            pltpu.VMEM((inner, width), BF16),
            dma((2,)),
            dma((DOWN_HOPS, DOWN_CHUNKS)),
            dma((DOWN_HOPS, DOWN_CHUNKS)),
            dma((UP_HOPS, UP_CHUNKS)),
            dma((UP_HOPS, UP_CHUNKS)),
            dma((2, 2)),
            dma((2, 2)),
            dma((3,)),
            dma((3,)),
            dma((4,)),
            dma((4,)),
        ],
        compiler_params=pltpu.CompilerParams(
            collective_id=0, has_side_effects=True, vmem_limit_bytes=53 << 20
        ),
        name="front_product",
    )(sigma_aa, l_as, block_mask)


def solution(mesh):
    placed = (P(("fr", "row"), "col"), P(("fr", "row"), "col"), P(("fr", "row"), "col"))
    return jax.shard_map(
        body, mesh=mesh, in_specs=placed, out_specs=P(("fr", "row"), "col"), check_vma=False
    )
```

```python
import functools

import jax
import jax.numpy as jnp
from jax import lax
from jax.experimental import pallas as pl
from jax.experimental.pallas import tpu as pltpu
from jax.sharding import PartitionSpec as P

MESH = pl.DeviceIdType.MESH
F32, BF16 = jnp.float32, jnp.bfloat16

NZ = 16
TURNS = 8
DOWN_HOPS, UP_HOPS = TURNS - 1, NZ - 1
DOWN_PIECES = (
    (384, 104, True), (488, 104, True), (288, 96, False), (192, 96, False), (96, 96, False), (0, 96, False),
)
UP_PIECES = (
    (384, 104, True), (488, 104, True), (592, 48, False), (640, 48, False), (688, 40, False), (728, 40, False),
)
CLIMB_SHARE = 5 / 16
DOWN_LATE = 120
TILE_GAP = 25
TILE = 128
AT_Y, AT_X, AT_PAIR = (0.14, 0.28), (0.75, 0.755, 0.76), 0.78


def climbs(block):
    return ((block < 5) & (block % 2 == 0)) | (block == 9) | (block == 11)


def split(value):
    high = value.astype(BF16)
    return high, (value - high.astype(F32)).astype(BF16)


def kernel(
    sigma_hbm, factor_hbm, mask_ref, out_ref,
    own, other, relay, factor, blocks, passing, rhs_high, rhs_low,
    load_sem, below_sem, peer_sem, down_send, down_recv, up_send, up_recv,
    y_send, y_recv, x_send, x_recv, pair_send, pair_recv,
):
    rows, inner = sigma_hbm.shape
    half = rows // 2
    z, col, fr = lax.axis_index("row"), lax.axis_index("col"), lax.axis_index("fr")
    core, x, y = col % 2, (col // 2) % 4, (col // 8) * 2 + fr

    def at_z(step):
        return ((z + step + NZ) % NZ, col, fr)

    def at_x(step):
        return (z, (col // 8) * 8 + ((x + step + 4) % 4) * 2 + core, fr)

    def at_y(step):
        there = (y + step + 4) % 4
        return (z, (there // 2) * 8 + x * 2 + core, there % 2)

    sibling = (z, col + 1 - 2 * core, fr)

    sigma_load = pltpu.make_async_copy(sigma_hbm, own.at[0], load_sem.at[0])
    factor_load = pltpu.make_async_copy(factor_hbm, factor, load_sem.at[1])
    factor_load.start()
    sigma_load.start()

    def entry(where):
        _, there, group = where
        place = (((there // 8) * 2 + group) * 4 + (there // 2) % 4) * 2 + there % 2
        return jnp.where((z == 0) & (place == 0), NZ * NZ, place)

    mine = entry((z, col, fr))
    peers = [(peer, entry(peer)) for peer in (at_y(-1), at_y(1), at_x(1), at_x(2), at_x(3), sibling)]
    earlier = sum((place < mine).astype(jnp.int32) for _, place in peers)

    def tell(semaphore, peer):
        pl.semaphore_signal(semaphore, inc=1, device_id=peer, device_id_type=MESH)

    barrier = pltpu.get_barrier_semaphore()
    tell(barrier, at_z(-1))
    for peer, place in peers:
        pl.when(place > mine)(functools.partial(tell, barrier, peer))

    def send(src, dst, send_sem, recv_sem, peer):
        return pltpu.make_async_remote_copy(
            src_ref=src, dst_ref=dst, send_sem=send_sem, recv_sem=recv_sem,
            device_id=peer, device_id_type=MESH,
        )

    def down_copy(step, piece):
        first, count, _ = DOWN_PIECES[piece]
        span = pl.ds(first, count)
        source = factor if step == 0 else blocks.at[step]
        return send(
            source.at[span], blocks.at[step + 1, span],
            down_send.at[step, piece], down_recv.at[step, piece], at_z(-1),
        )

    def climbed(step, span):
        if step <= UP_HOPS - TURNS:
            return passing.at[step, pl.ds(span.start - UP_PIECES[0][0], span.size)]
        return blocks.at[UP_HOPS - step, span]

    def up_copy(step, piece):
        first, count, _ = UP_PIECES[piece]
        span = pl.ds(first, count)
        source = factor.at[span] if step == 0 else climbed(step - 1, span)
        return send(
            source, climbed(step, span),
            up_send.at[step, piece], up_recv.at[step, piece], at_z(1),
        )

    def only_if(needed, condition, action):
        if needed:
            pl.when(condition)(action)
        else:
            action()

    def down_do(block_step, piece, action):
        only_if(DOWN_PIECES[piece][2], jnp.logical_not(climbs((z + block_step) % NZ)), action)

    def up_do(block_step, piece, action):
        only_if(UP_PIECES[piece][2], climbs((z + NZ - block_step) % NZ), action)

    def y_copy(leg, way):
        span = pl.ds(way * half, half)
        source = own.at[0, span] if leg == 0 else relay.at[way]
        target = relay.at[way] if leg == 0 else own.at[4, span]
        return send(source, target, y_send.at[leg, way], y_recv.at[leg, way], at_y(1 - 2 * way))

    def x_copy(distance):
        which = jnp.where(x >= distance, 0, 4)
        return send(own.at[which], own.at[distance], x_send.at[distance - 1], x_recv.at[distance - 1], at_x(-distance))

    def pair_copy(distance):
        slot = distance - 1 + core
        return send(own.at[distance], other.at[slot], pair_send.at[slot], pair_recv.at[slot], sibling)

    def pair_arrival(slot):
        return send(other.at[slot], other.at[slot], pair_send.at[slot], pair_recv.at[slot], sibling)

    def multiply(tile, turn, low_row=0, high_row=None):
        high_row = inner if high_row is None else high_row
        depth = high_row - low_row
        if tile == 0:
            source = factor if turn == 0 else blocks.at[turn]
            high, low = split(source[pl.ds(low_row, depth)])
            rhs_high[pl.ds(0, depth)] = high
            rhs_low[pl.ds(0, depth)] = low
        span = pl.ds(tile * TILE, TILE)
        lhs = own if turn % 2 == 0 else other
        high, low = split(lhs[turn // 2, span, pl.ds(low_row, depth)])
        dot = functools.partial(jnp.dot, preferred_element_type=F32)
        one, two = rhs_high[pl.ds(0, depth)], rhs_low[pl.ds(0, depth)]
        value = dot(high, one) + (dot(high, two) + dot(low, one))
        out_ref[span] = -value if turn == 0 else out_ref[span] - value

    factor_load.wait()
    factor[...] = factor[...] * mask_ref[0, 0].astype(F32)
    sigma_load.wait()
    pl.semaphore_wait(barrier, 1 + earlier)
    tell(below_sem, at_z(1))
    for piece in range(len(UP_PIECES)):
        up_do(0, piece, up_copy(0, piece).start)
    for peer, place in peers:
        pl.when(place < mine)(functools.partial(tell, peer_sem, peer))
    pl.semaphore_wait(below_sem, 1)
    for piece in range(len(DOWN_PIECES)):
        down_do(0, piece, down_copy(0, piece).start)

    @pl.when(earlier < len(peers))
    def _():
        pl.semaphore_wait(peer_sem, len(peers) - earlier)

    for way in range(2):
        y_copy(0, way).start()
    for distance in (1, 3, 2):

        @pl.when(x >= distance)
        def _():
            x_copy(distance).start()

    @pl.when(core == 1)
    def _():
        pair_copy(0).start()

    for tile in range(rows // TILE):
        multiply(tile, 0)

    def down_event(step, piece):
        def action():
            down_copy(step, piece).wait_recv()
            if step + 1 < DOWN_HOPS:
                down_copy(step + 1, piece).start()

        down_do(step + 1, piece, action)

    def up_event(step, piece):
        def action():
            up_copy(step, piece).wait_recv()
            if step + 1 < UP_HOPS:
                up_copy(step + 1, piece).start()

        up_do(step + 1, piece, action)

    def y_event(leg):
        for way in range(2):
            y_copy(leg, way).wait_recv()
            if leg == 0:
                y_copy(1, way).start()
        if leg == 1:
            for distance in (1, 3, 2):

                @pl.when(x < distance)
                def _():
                    x_copy(distance).start()

            @pl.when(core == 0)
            def _():
                pair_copy(4).start()

    def x_event(distance):
        x_copy(distance).wait_recv()
        pair_copy(distance).start()

    def pair_event():
        for slot in range(4):
            pair_arrival(slot).wait_recv()

    def arrivals(pieces, share, hops):
        sizes = [count * (share if either else 1) for _, count, either in pieces]
        return [[step * sum(sizes) + sum(sizes[: piece + 1]) for piece in range(len(sizes))] for step in range(hops)]

    down_times = arrivals(DOWN_PIECES, 1 - CLIMB_SHARE, DOWN_HOPS)
    up_times = arrivals(UP_PIECES, CLIMB_SHARE, UP_HOPS)
    whole = max(down_times[-1][-1], up_times[-1][-1])
    events = [(AT_Y[leg] * whole, functools.partial(y_event, leg)) for leg in range(2)]
    events += [(when * whole, functools.partial(x_event, distance)) for when, distance in zip(AT_X, (1, 3, 2))]
    events += [(AT_PAIR * whole, pair_event)]
    down_times = [[min(when + DOWN_LATE, max(when, whole - 0.1 * (len(row) - 1 - piece))) for piece, when in enumerate(row)] for row in down_times]
    for times, event in ((down_times, down_event), (up_times, up_event)):
        for step, row in enumerate(times):
            for piece, when in enumerate(row):
                events.append((when, functools.partial(event, step, piece)))
    products = [
        (up_times[-1][1], 1, 0, 512), (up_times[-1][-1], 1, 512, inner),
        (down_times[-1][3], TURNS - 1, 256, inner), (down_times[-1][-1], TURNS - 1, 0, 256),
    ]
    for turn in range(2, TURNS - 1):
        products.append((max(down_times[turn - 1][-1], up_times[UP_HOPS - turn][-1]), turn, 0, inner))
    free = AT_PAIR * whole
    for when, *product in sorted(products):
        for tile in range(rows // TILE):
            free = max(when, free) + 0.01
            events.append((free, functools.partial(multiply, tile, *product)))
            free += TILE_GAP
    for _, event in sorted(events, key=lambda entry: entry[0]):
        event()

    for step in range(DOWN_HOPS):
        for piece in range(len(DOWN_PIECES)):
            down_do(step, piece, down_copy(step, piece).wait_send)
    for step in range(UP_HOPS):
        for piece in range(len(UP_PIECES)):
            up_do(step, piece, up_copy(step, piece).wait_send)
    for leg in range(2):
        for way in range(2):
            y_copy(leg, way).wait_send()
    for distance in (1, 2, 3):
        x_copy(distance).wait_send()
    for slot in range(4):
        pair_arrival(slot).wait_send()


def body(sigma_aa, l_as, block_mask):
    rows, inner = sigma_aa.shape
    width = l_as.shape[1]
    dma = pltpu.SemaphoreType.DMA
    return pl.pallas_call(
        kernel,
        out_shape=jax.ShapeDtypeStruct((rows, width), F32),
        in_specs=[
            pl.BlockSpec(memory_space=pltpu.HBM),
            pl.BlockSpec(memory_space=pltpu.HBM),
            pl.BlockSpec(memory_space=pltpu.SMEM),
        ],
        out_specs=pl.BlockSpec(memory_space=pltpu.VMEM),
        scratch_shapes=[
            pltpu.VMEM((5, rows, inner), F32),
            pltpu.VMEM((4, rows, inner), F32),
            pltpu.VMEM((2, rows // 2, inner), F32),
            pltpu.VMEM((inner, width), F32),
            pltpu.VMEM((TURNS, inner, width), F32),
            pltpu.VMEM((UP_HOPS - TURNS + 1, inner - UP_PIECES[0][0], width), F32),
            pltpu.VMEM((inner, width), BF16),
            pltpu.VMEM((inner, width), BF16),
            dma((2,)),
            pltpu.SemaphoreType.REGULAR,
            pltpu.SemaphoreType.REGULAR,
            dma((DOWN_HOPS, len(DOWN_PIECES))),
            dma((DOWN_HOPS, len(DOWN_PIECES))),
            dma((UP_HOPS, len(UP_PIECES))),
            dma((UP_HOPS, len(UP_PIECES))),
            dma((2, 2)),
            dma((2, 2)),
            dma((3,)),
            dma((3,)),
            dma((4,)),
            dma((4,)),
        ],
        compiler_params=pltpu.CompilerParams(
            collective_id=0, has_side_effects=True, vmem_limit_bytes=53 << 20
        ),
        name="front_product",
    )(sigma_aa, l_as, block_mask)


def solution(mesh):
    placed = (P(("fr", "row"), "col"), P(("fr", "row"), "col"), P(("fr", "row"), "col"))
    return jax.shard_map(
        body, mesh=mesh, in_specs=placed, out_specs=P(("fr", "row"), "col"), check_vma=False
    )
```

```python
import functools

import jax
import jax.numpy as jnp
from jax import lax
from jax.experimental import pallas as pl
from jax.experimental.pallas import tpu as pltpu
from jax.sharding import PartitionSpec as P

MESH = pl.DeviceIdType.MESH
F32, BF16 = jnp.float32, jnp.bfloat16

NZ = 16
TURNS = 8
DOWN_HOPS, UP_HOPS = TURNS - 1, NZ - 1
DOWN_PIECES = (
    (440, 80, True), (520, 80, True), (328, 112, False), (216, 112, False), (112, 104, False), (0, 112, False),
)
UP_PIECES = ((440, 80, True), (520, 80, True), (600, 56, False), (656, 56, False), (712, 56, False))
CLIMB_SHARE = 7 / 16
DOWN_LATE = 60
TILE_GAP = 25
TILE = 128
AT_Y, AT_X, AT_PAIR = (0.14, 0.28), (0.75, 0.755, 0.76), 0.78


def climbs(block):
    even = block % 2 == 0
    return ((block < 7) & even) | ((block > 8) & (block < 14) & jnp.logical_not(even))


def split(value):
    high = value.astype(BF16)
    return high, (value - high.astype(F32)).astype(BF16)


def kernel(
    sigma_hbm, factor_hbm, mask_ref, out_ref,
    own, other, relay, factor, blocks, passing, rhs_high, rhs_low,
    load_sem, below_sem, peer_sem, down_send, down_recv, up_send, up_recv,
    y_send, y_recv, x_send, x_recv, pair_send, pair_recv,
):
    rows, inner = sigma_hbm.shape
    half = rows // 2
    z, col, fr = lax.axis_index("row"), lax.axis_index("col"), lax.axis_index("fr")
    core, x, y = col % 2, (col // 2) % 4, (col // 8) * 2 + fr

    def at_z(step):
        return ((z + step + NZ) % NZ, col, fr)

    def at_x(step):
        return (z, (col // 8) * 8 + ((x + step + 4) % 4) * 2 + core, fr)

    def at_y(step):
        there = (y + step + 4) % 4
        return (z, (there // 2) * 8 + x * 2 + core, there % 2)

    sibling = (z, col + 1 - 2 * core, fr)

    sigma_load = pltpu.make_async_copy(sigma_hbm, own.at[0], load_sem.at[0])
    factor_load = pltpu.make_async_copy(factor_hbm, factor, load_sem.at[1])
    factor_load.start()
    sigma_load.start()

    def entry(where):
        _, there, group = where
        place = (((there // 8) * 2 + group) * 4 + (there // 2) % 4) * 2 + there % 2
        return jnp.where((z == 0) & (place == 0), NZ * NZ, place)

    mine = entry((z, col, fr))
    peers = [(peer, entry(peer)) for peer in (at_y(-1), at_y(1), at_x(1), at_x(2), at_x(3), sibling)]
    earlier = sum((place < mine).astype(jnp.int32) for _, place in peers)

    def tell(semaphore, peer):
        pl.semaphore_signal(semaphore, inc=1, device_id=peer, device_id_type=MESH)

    barrier = pltpu.get_barrier_semaphore()
    tell(barrier, at_z(-1))
    for peer, place in peers:
        pl.when(place > mine)(functools.partial(tell, barrier, peer))

    def send(src, dst, send_sem, recv_sem, peer):
        return pltpu.make_async_remote_copy(
            src_ref=src, dst_ref=dst, send_sem=send_sem, recv_sem=recv_sem,
            device_id=peer, device_id_type=MESH,
        )

    def down_copy(step, piece):
        first, count, _ = DOWN_PIECES[piece]
        span = pl.ds(first, count)
        source = factor if step == 0 else blocks.at[step]
        return send(
            source.at[span], blocks.at[step + 1, span],
            down_send.at[step, piece], down_recv.at[step, piece], at_z(-1),
        )

    def climbed(step, span):
        if step <= UP_HOPS - TURNS:
            return passing.at[step, pl.ds(span.start - UP_PIECES[0][0], span.size)]
        return blocks.at[UP_HOPS - step, span]

    def up_copy(step, piece):
        first, count, _ = UP_PIECES[piece]
        span = pl.ds(first, count)
        source = factor.at[span] if step == 0 else climbed(step - 1, span)
        return send(
            source, climbed(step, span),
            up_send.at[step, piece], up_recv.at[step, piece], at_z(1),
        )

    def only_if(needed, condition, action):
        if needed:
            pl.when(condition)(action)
        else:
            action()

    def down_do(block_step, piece, action):
        only_if(DOWN_PIECES[piece][2], jnp.logical_not(climbs((z + block_step) % NZ)), action)

    def up_do(block_step, piece, action):
        only_if(UP_PIECES[piece][2], climbs((z + NZ - block_step) % NZ), action)

    def y_copy(leg, way):
        span = pl.ds(way * half, half)
        source = own.at[0, span] if leg == 0 else relay.at[way]
        target = relay.at[way] if leg == 0 else own.at[4, span]
        return send(source, target, y_send.at[leg, way], y_recv.at[leg, way], at_y(1 - 2 * way))

    def x_copy(distance):
        which = jnp.where(x >= distance, 0, 4)
        return send(own.at[which], own.at[distance], x_send.at[distance - 1], x_recv.at[distance - 1], at_x(-distance))

    def pair_copy(distance):
        slot = distance - 1 + core
        return send(own.at[distance], other.at[slot], pair_send.at[slot], pair_recv.at[slot], sibling)

    def pair_arrival(slot):
        return send(other.at[slot], other.at[slot], pair_send.at[slot], pair_recv.at[slot], sibling)

    def multiply(tile, turn, low_row=0, high_row=None):
        high_row = inner if high_row is None else high_row
        depth = high_row - low_row
        if tile == 0:
            source = factor if turn == 0 else blocks.at[turn]
            high, low = split(source[pl.ds(low_row, depth)])
            rhs_high[pl.ds(0, depth)] = high
            rhs_low[pl.ds(0, depth)] = low
        span = pl.ds(tile * TILE, TILE)
        lhs = own if turn % 2 == 0 else other
        high, low = split(lhs[turn // 2, span, pl.ds(low_row, depth)])
        dot = functools.partial(jnp.dot, preferred_element_type=F32)
        one, two = rhs_high[pl.ds(0, depth)], rhs_low[pl.ds(0, depth)]
        value = dot(high, one) + (dot(high, two) + dot(low, one))
        out_ref[span] = -value if turn == 0 else out_ref[span] - value

    factor_load.wait()
    factor[...] = factor[...] * mask_ref[0, 0].astype(F32)
    sigma_load.wait()
    pl.semaphore_wait(barrier, 1 + earlier)
    tell(below_sem, at_z(1))
    for piece in range(len(UP_PIECES)):
        up_do(0, piece, up_copy(0, piece).start)
    for peer, place in peers:
        pl.when(place < mine)(functools.partial(tell, peer_sem, peer))
    pl.semaphore_wait(below_sem, 1)
    for piece in range(len(DOWN_PIECES)):
        down_do(0, piece, down_copy(0, piece).start)

    @pl.when(earlier < len(peers))
    def _():
        pl.semaphore_wait(peer_sem, len(peers) - earlier)

    for way in range(2):
        y_copy(0, way).start()
    for distance in (1, 3, 2):

        @pl.when(x >= distance)
        def _():
            x_copy(distance).start()

    @pl.when(core == 1)
    def _():
        pair_copy(0).start()

    for tile in range(rows // TILE):
        multiply(tile, 0)

    def down_event(step, piece):
        def action():
            down_copy(step, piece).wait_recv()
            if step + 1 < DOWN_HOPS:
                down_copy(step + 1, piece).start()

        down_do(step + 1, piece, action)

    def up_event(step, piece):
        def action():
            up_copy(step, piece).wait_recv()
            if step + 1 < UP_HOPS:
                up_copy(step + 1, piece).start()

        up_do(step + 1, piece, action)

    def y_event(leg):
        for way in range(2):
            y_copy(leg, way).wait_recv()
            if leg == 0:
                y_copy(1, way).start()
        if leg == 1:
            for distance in (1, 3, 2):

                @pl.when(x < distance)
                def _():
                    x_copy(distance).start()

            @pl.when(core == 0)
            def _():
                pair_copy(4).start()

    def x_event(distance):
        x_copy(distance).wait_recv()
        pair_copy(distance).start()

    def pair_event():
        for slot in range(4):
            pair_arrival(slot).wait_recv()

    def arrivals(pieces, share, hops):
        sizes = [count * (share if either else 1) for _, count, either in pieces]
        return [[step * sum(sizes) + sum(sizes[: piece + 1]) for piece in range(len(sizes))] for step in range(hops)]

    down_times = arrivals(DOWN_PIECES, 1 - CLIMB_SHARE, DOWN_HOPS)
    up_times = arrivals(UP_PIECES, CLIMB_SHARE, UP_HOPS)
    whole = max(down_times[-1][-1], up_times[-1][-1])
    events = [(AT_Y[leg] * whole, functools.partial(y_event, leg)) for leg in range(2)]
    events += [(when * whole, functools.partial(x_event, distance)) for when, distance in zip(AT_X, (1, 3, 2))]
    events += [(AT_PAIR * whole, pair_event)]
    down_times = [[min(when + DOWN_LATE, max(when, whole - 0.1 * (len(row) - 1 - piece))) for piece, when in enumerate(row)] for row in down_times]
    for times, event in ((down_times, down_event), (up_times, up_event)):
        for step, row in enumerate(times):
            for piece, when in enumerate(row):
                events.append((when, functools.partial(event, step, piece)))
    products = [
        (up_times[-1][1], 1, 0, 512), (up_times[-1][-1], 1, 512, inner),
        (down_times[-1][3], TURNS - 1, 256, inner), (down_times[-1][-1], TURNS - 1, 0, 256),
    ]
    for turn in range(2, TURNS - 1):
        products.append((max(down_times[turn - 1][-1], up_times[UP_HOPS - turn][-1]), turn, 0, inner))
    free = AT_PAIR * whole
    for when, *product in sorted(products):
        for tile in range(rows // TILE):
            free = max(when, free) + 0.01
            events.append((free, functools.partial(multiply, tile, *product)))
            free += TILE_GAP
    for _, event in sorted(events, key=lambda entry: entry[0]):
        event()

    for step in range(DOWN_HOPS):
        for piece in range(len(DOWN_PIECES)):
            down_do(step, piece, down_copy(step, piece).wait_send)
    for step in range(UP_HOPS):
        for piece in range(len(UP_PIECES)):
            up_do(step, piece, up_copy(step, piece).wait_send)
    for leg in range(2):
        for way in range(2):
            y_copy(leg, way).wait_send()
    for distance in (1, 2, 3):
        x_copy(distance).wait_send()
    for slot in range(4):
        pair_arrival(slot).wait_send()


def body(sigma_aa, l_as, block_mask):
    rows, inner = sigma_aa.shape
    width = l_as.shape[1]
    dma = pltpu.SemaphoreType.DMA
    return pl.pallas_call(
        kernel,
        out_shape=jax.ShapeDtypeStruct((rows, width), F32),
        in_specs=[
            pl.BlockSpec(memory_space=pltpu.HBM),
            pl.BlockSpec(memory_space=pltpu.HBM),
            pl.BlockSpec(memory_space=pltpu.SMEM),
        ],
        out_specs=pl.BlockSpec(memory_space=pltpu.VMEM),
        scratch_shapes=[
            pltpu.VMEM((5, rows, inner), F32),
            pltpu.VMEM((4, rows, inner), F32),
            pltpu.VMEM((2, rows // 2, inner), F32),
            pltpu.VMEM((inner, width), F32),
            pltpu.VMEM((TURNS, inner, width), F32),
            pltpu.VMEM((UP_HOPS - TURNS + 1, inner - UP_PIECES[0][0], width), F32),
            pltpu.VMEM((inner, width), BF16),
            pltpu.VMEM((inner, width), BF16),
            dma((2,)),
            pltpu.SemaphoreType.REGULAR,
            pltpu.SemaphoreType.REGULAR,
            dma((DOWN_HOPS, len(DOWN_PIECES))),
            dma((DOWN_HOPS, len(DOWN_PIECES))),
            dma((UP_HOPS, len(UP_PIECES))),
            dma((UP_HOPS, len(UP_PIECES))),
            dma((2, 2)),
            dma((2, 2)),
            dma((3,)),
            dma((3,)),
            dma((4,)),
            dma((4,)),
        ],
        compiler_params=pltpu.CompilerParams(
            collective_id=0, has_side_effects=True, vmem_limit_bytes=53 << 20
        ),
        name="front_product",
    )(sigma_aa, l_as, block_mask)


def solution(mesh):
    placed = (P(("fr", "row"), "col"), P(("fr", "row"), "col"), P(("fr", "row"), "col"))
    return jax.shard_map(
        body, mesh=mesh, in_specs=placed, out_specs=P(("fr", "row"), "col"), check_vma=False
    )
```

```python
import functools

import jax
import jax.numpy as jnp
from jax import lax
from jax.experimental import pallas as pl
from jax.experimental.pallas import tpu as pltpu
from jax.sharding import PartitionSpec as P

MESH = pl.DeviceIdType.MESH
F32, BF16 = jnp.float32, jnp.bfloat16

NZ = 16
TURNS = 8
DOWN_HOPS, UP_HOPS = TURNS - 1, NZ - 1
DOWN_PIECES = (
    (440, 80, True), (520, 80, True), (328, 112, False), (216, 112, False), (112, 104, False), (0, 112, False),
)
UP_PIECES = ((440, 80, True), (520, 80, True), (600, 56, False), (656, 56, False), (712, 56, False))
CLIMB_SHARE = 7 / 16
DOWN_LATE = 90
TILE_GAP = 10
TILE = 128
AT_Y, AT_X, AT_PAIR = (0.14, 0.28), (0.75, 0.755, 0.76), 0.78


def climbs(block):
    even = block % 2 == 0
    return ((block < 7) & even) | ((block > 8) & (block < 14) & jnp.logical_not(even))


def split(value):
    high = value.astype(BF16)
    return high, (value - high.astype(F32)).astype(BF16)


def kernel(
    sigma_hbm, factor_hbm, mask_ref, out_ref,
    own, other, relay, factor, blocks, passing, rhs_high, rhs_low,
    load_sem, below_sem, peer_sem, down_send, down_recv, up_send, up_recv,
    y_send, y_recv, x_send, x_recv, pair_send, pair_recv,
):
    rows, inner = sigma_hbm.shape
    half = rows // 2
    z, col, fr = lax.axis_index("row"), lax.axis_index("col"), lax.axis_index("fr")
    core, x, y = col % 2, (col // 2) % 4, (col // 8) * 2 + fr

    def at_z(step):
        return ((z + step + NZ) % NZ, col, fr)

    def at_x(step):
        return (z, (col // 8) * 8 + ((x + step + 4) % 4) * 2 + core, fr)

    def at_y(step):
        there = (y + step + 4) % 4
        return (z, (there // 2) * 8 + x * 2 + core, there % 2)

    sibling = (z, col + 1 - 2 * core, fr)

    sigma_load = pltpu.make_async_copy(sigma_hbm, own.at[0], load_sem.at[0])
    factor_load = pltpu.make_async_copy(factor_hbm, factor, load_sem.at[1])
    factor_load.start()
    sigma_load.start()

    def entry(where):
        _, there, group = where
        place = (((there // 8) * 2 + group) * 4 + (there // 2) % 4) * 2 + there % 2
        return jnp.where((z == 0) & (place == 0), NZ * NZ, place)

    mine = entry((z, col, fr))
    peers = [(peer, entry(peer)) for peer in (at_y(-1), at_y(1), at_x(1), at_x(2), at_x(3), sibling)]
    earlier = sum((place < mine).astype(jnp.int32) for _, place in peers)

    def tell(semaphore, peer):
        pl.semaphore_signal(semaphore, inc=1, device_id=peer, device_id_type=MESH)

    barrier = pltpu.get_barrier_semaphore()
    tell(barrier, at_z(-1))
    for peer, place in peers:
        pl.when(place > mine)(functools.partial(tell, barrier, peer))

    def send(src, dst, send_sem, recv_sem, peer):
        return pltpu.make_async_remote_copy(
            src_ref=src, dst_ref=dst, send_sem=send_sem, recv_sem=recv_sem,
            device_id=peer, device_id_type=MESH,
        )

    def down_copy(step, piece):
        first, count, _ = DOWN_PIECES[piece]
        span = pl.ds(first, count)
        source = factor if step == 0 else blocks.at[step]
        return send(
            source.at[span], blocks.at[step + 1, span],
            down_send.at[step, piece], down_recv.at[step, piece], at_z(-1),
        )

    def climbed(step, span):
        if step <= UP_HOPS - TURNS:
            return passing.at[step, pl.ds(span.start - UP_PIECES[0][0], span.size)]
        return blocks.at[UP_HOPS - step, span]

    def up_copy(step, piece):
        first, count, _ = UP_PIECES[piece]
        span = pl.ds(first, count)
        source = factor.at[span] if step == 0 else climbed(step - 1, span)
        return send(
            source, climbed(step, span),
            up_send.at[step, piece], up_recv.at[step, piece], at_z(1),
        )

    def only_if(needed, condition, action):
        if needed:
            pl.when(condition)(action)
        else:
            action()

    def down_do(block_step, piece, action):
        only_if(DOWN_PIECES[piece][2], jnp.logical_not(climbs((z + block_step) % NZ)), action)

    def up_do(block_step, piece, action):
        only_if(UP_PIECES[piece][2], climbs((z + NZ - block_step) % NZ), action)

    def y_copy(leg, way):
        span = pl.ds(way * half, half)
        source = own.at[0, span] if leg == 0 else relay.at[way]
        target = relay.at[way] if leg == 0 else own.at[4, span]
        return send(source, target, y_send.at[leg, way], y_recv.at[leg, way], at_y(1 - 2 * way))

    def x_copy(distance):
        which = jnp.where(x >= distance, 0, 4)
        return send(own.at[which], own.at[distance], x_send.at[distance - 1], x_recv.at[distance - 1], at_x(-distance))

    def pair_copy(distance):
        slot = distance - 1 + core
        return send(own.at[distance], other.at[slot], pair_send.at[slot], pair_recv.at[slot], sibling)

    def pair_arrival(slot):
        return send(other.at[slot], other.at[slot], pair_send.at[slot], pair_recv.at[slot], sibling)

    def multiply(tile, turn, low_row=0, high_row=None):
        high_row = inner if high_row is None else high_row
        depth = high_row - low_row
        if tile == 0:
            source = factor if turn == 0 else blocks.at[turn]
            high, low = split(source[pl.ds(low_row, depth)])
            rhs_high[pl.ds(0, depth)] = high
            rhs_low[pl.ds(0, depth)] = low
        span = pl.ds(tile * TILE, TILE)
        lhs = own if turn % 2 == 0 else other
        high, low = split(lhs[turn // 2, span, pl.ds(low_row, depth)])
        dot = functools.partial(jnp.dot, preferred_element_type=F32)
        one, two = rhs_high[pl.ds(0, depth)], rhs_low[pl.ds(0, depth)]
        value = dot(high, one) + (dot(high, two) + dot(low, one))
        out_ref[span] = -value if turn == 0 else out_ref[span] - value

    factor_load.wait()
    factor[...] = factor[...] * mask_ref[0, 0].astype(F32)
    sigma_load.wait()
    pl.semaphore_wait(barrier, 1 + earlier)
    tell(below_sem, at_z(1))
    for piece in range(len(UP_PIECES)):
        up_do(0, piece, up_copy(0, piece).start)
    for peer, place in peers:
        pl.when(place < mine)(functools.partial(tell, peer_sem, peer))
    pl.semaphore_wait(below_sem, 1)
    for piece in range(len(DOWN_PIECES)):
        down_do(0, piece, down_copy(0, piece).start)

    @pl.when(earlier < len(peers))
    def _():
        pl.semaphore_wait(peer_sem, len(peers) - earlier)

    for way in range(2):
        y_copy(0, way).start()
    for distance in (1, 3, 2):

        @pl.when(x >= distance)
        def _():
            x_copy(distance).start()

    @pl.when(core == 1)
    def _():
        pair_copy(0).start()

    for tile in range(rows // TILE):
        multiply(tile, 0)

    def down_event(step, piece):
        def action():
            down_copy(step, piece).wait_recv()
            if step + 1 < DOWN_HOPS:
                down_copy(step + 1, piece).start()

        down_do(step + 1, piece, action)

    def up_event(step, piece):
        def action():
            up_copy(step, piece).wait_recv()
            if step + 1 < UP_HOPS:
                up_copy(step + 1, piece).start()

        up_do(step + 1, piece, action)

    def y_event(leg):
        for way in range(2):
            y_copy(leg, way).wait_recv()
            if leg == 0:
                y_copy(1, way).start()
        if leg == 1:
            for distance in (1, 3, 2):

                @pl.when(x < distance)
                def _():
                    x_copy(distance).start()

            @pl.when(core == 0)
            def _():
                pair_copy(4).start()

    def x_event(distance):
        x_copy(distance).wait_recv()
        pair_copy(distance).start()

    def pair_event():
        for slot in range(4):
            pair_arrival(slot).wait_recv()

    def arrivals(pieces, share, hops):
        sizes = [count * (share if either else 1) for _, count, either in pieces]
        return [[step * sum(sizes) + sum(sizes[: piece + 1]) for piece in range(len(sizes))] for step in range(hops)]

    down_times = arrivals(DOWN_PIECES, 1 - CLIMB_SHARE, DOWN_HOPS)
    up_times = arrivals(UP_PIECES, CLIMB_SHARE, UP_HOPS)
    whole = max(down_times[-1][-1], up_times[-1][-1])
    events = [(AT_Y[leg] * whole, functools.partial(y_event, leg)) for leg in range(2)]
    events += [(when * whole, functools.partial(x_event, distance)) for when, distance in zip(AT_X, (1, 3, 2))]
    events += [(AT_PAIR * whole, pair_event)]
    down_times = [[min(when + DOWN_LATE, max(when, whole - 0.1 * (len(row) - 1 - piece))) for piece, when in enumerate(row)] for row in down_times]
    for times, event in ((down_times, down_event), (up_times, up_event)):
        for step, row in enumerate(times):
            for piece, when in enumerate(row):
                events.append((when, functools.partial(event, step, piece)))
    products = [
        (up_times[-1][1], 1, 0, 512), (up_times[-1][-1], 1, 512, inner),
        (down_times[-1][3], TURNS - 1, 256, inner), (down_times[-1][-1], TURNS - 1, 0, 256),
    ]
    for turn in range(2, TURNS - 1):
        products.append((max(down_times[turn - 1][-1], up_times[UP_HOPS - turn][-1]), turn, 0, inner))
    free = AT_PAIR * whole
    for when, *product in sorted(products):
        for tile in range(rows // TILE):
            free = max(when, free) + 0.01
            events.append((free, functools.partial(multiply, tile, *product)))
            free += TILE_GAP
    for _, event in sorted(events, key=lambda entry: entry[0]):
        event()

    for step in range(DOWN_HOPS):
        for piece in range(len(DOWN_PIECES)):
            down_do(step, piece, down_copy(step, piece).wait_send)
    for step in range(UP_HOPS):
        for piece in range(len(UP_PIECES)):
            up_do(step, piece, up_copy(step, piece).wait_send)
    for leg in range(2):
        for way in range(2):
            y_copy(leg, way).wait_send()
    for distance in (1, 2, 3):
        x_copy(distance).wait_send()
    for slot in range(4):
        pair_arrival(slot).wait_send()


def body(sigma_aa, l_as, block_mask):
    rows, inner = sigma_aa.shape
    width = l_as.shape[1]
    dma = pltpu.SemaphoreType.DMA
    return pl.pallas_call(
        kernel,
        out_shape=jax.ShapeDtypeStruct((rows, width), F32),
        in_specs=[
            pl.BlockSpec(memory_space=pltpu.HBM),
            pl.BlockSpec(memory_space=pltpu.HBM),
            pl.BlockSpec(memory_space=pltpu.SMEM),
        ],
        out_specs=pl.BlockSpec(memory_space=pltpu.VMEM),
        scratch_shapes=[
            pltpu.VMEM((5, rows, inner), F32),
            pltpu.VMEM((4, rows, inner), F32),
            pltpu.VMEM((2, rows // 2, inner), F32),
            pltpu.VMEM((inner, width), F32),
            pltpu.VMEM((TURNS, inner, width), F32),
            pltpu.VMEM((UP_HOPS - TURNS + 1, inner - UP_PIECES[0][0], width), F32),
            pltpu.VMEM((inner, width), BF16),
            pltpu.VMEM((inner, width), BF16),
            dma((2,)),
            pltpu.SemaphoreType.REGULAR,
            pltpu.SemaphoreType.REGULAR,
            dma((DOWN_HOPS, len(DOWN_PIECES))),
            dma((DOWN_HOPS, len(DOWN_PIECES))),
            dma((UP_HOPS, len(UP_PIECES))),
            dma((UP_HOPS, len(UP_PIECES))),
            dma((2, 2)),
            dma((2, 2)),
            dma((3,)),
            dma((3,)),
            dma((4,)),
            dma((4,)),
        ],
        compiler_params=pltpu.CompilerParams(
            collective_id=0, has_side_effects=True, vmem_limit_bytes=53 << 20
        ),
        name="front_product",
    )(sigma_aa, l_as, block_mask)


def solution(mesh):
    placed = (P(("fr", "row"), "col"), P(("fr", "row"), "col"), P(("fr", "row"), "col"))
    return jax.shard_map(
        body, mesh=mesh, in_specs=placed, out_specs=P(("fr", "row"), "col"), check_vma=False
    )
```
